256 devices in a mesh: seq: 16 (over z_hi, y), head: 4 (over x), prompt: 4 (over z_lo, core).
Axes of the slice: x: 4, y: 4, z: 8 (z_hi: 4, z_lo: 2; z = z_hi * 2 + z_lo), core: 2. Of those that a mesh axis runs over, the one named last changes fastest.
Arguments:
- heads_pre: bfloat16 [8192, 16384], P(('prompt', 'seq'), 'head'), parts along dimension 0, may hold values from -6 to 6
- maps_pre: bfloat16 [8192, 2, 2048], P(('prompt', 'seq'), None, 'head'), parts along dimension 0, may hold values from -6 to 6
- step_prompt: float32 [8192, 256], P(('prompt', 'seq'), 'head'), parts along dimension 0, may hold values from 0 to 0.3, as said below
- head_rate: float32 [256], P('head'), may hold values from 0.5 to 1
- skip_gain: float32 [256], P('head'), may hold values from 0.5 to 1.5
- conv_head_taps: float32 [4, 16384], P(None, 'head'), may hold values from -3 to 3
- conv_head_bias: float32 [16384], P('head'), may hold values from -3 to 3
- conv_map_taps: float32 [4, 2, 2048], P(None, None, 'head'), may hold values from -3 to 3
- filter_mapping_offset: float32 [2, 2048], P(None, 'head'), may hold values from -3 to 3
- heads_dec: bfloat16 [64, 4, 16384], P(('prompt', 'seq'), None, 'head'), parts along dimension 0, may hold values from -6 to 6
- maps_dec: bfloat16 [64, 4, 2, 2048], P(('prompt', 'seq'), None, None, 'head'), parts along dimension 0, may hold values from -6 to 6
- step_dec: float32 [64, 4, 256], P(('prompt', 'seq'), None, 'head'), parts along dimension 0, may hold values from 0.01 to 0.3
Outputs:
- prompt_out: bfloat16 [8192, 16384], P(('prompt', 'seq'), 'head'), parts along dimension 0
- sample_out: bfloat16 [64, 4, 16384], P(('prompt', 'seq'), None, 'head'), parts along dimension 0
The draws below stay inside these ranges and needn't reach their ends.
There are 4 independent parts, one for each index of `prompt`. The reference program is written for one: setup_inputs(seed, part) draws one part's arguments, and reference() takes and returns one part's arrays. A program takes and returns all parts, laid end to end along the dimension named above; an argument that names none is the same for every part. Nothing has to cross between parts.
Inputs may be any that keep to these rules, and one draw needn't show every extreme that they name: `step_prompt`: step sizes, all positive.
All inputs are finite; a program needn't handle non-finite values.
Results may differ from the reference program's by a relative error of at most 0.0035.
Values may be sent and summed in bfloat16 or wider, within the bound.
A program may use at most 192 MiB of HBM per device.

```python
import math
import jax
import jax.numpy as jnp
from jax import lax

HEADS = 256
HEAD_DIM = 64
STATE = 256
GROUPS = 8
CONV = 4
BLOCK_TOKENS = 128
STEPS = 4
QUERY_WORDS = 2048
SAMPLES = 16


def draw_step_prompt(key, part):
    random_subkeys = jax.random.split(key, 5)
    slow_share = 0.5
    is_slow = jax.random.bernoulli(random_subkeys[0], slow_share, (HEADS,))
    spread = jax.random.uniform(random_subkeys[1], (HEADS,), jnp.float32)
    gradual_baseline = 0.05 / QUERY_WORDS * jnp.exp(spread * math.log(3.0))
    fast_base = 0.03 * jnp.exp(spread * math.log(3.0))
    jaggedness_level = jnp.exp(jax.random.uniform(random_subkeys[2], (QUERY_WORDS, HEADS), jnp.float32, math.log(0.5), math.log(2.0)))
    block_count = QUERY_WORDS // BLOCK_TOKENS
    quiet_factor = jnp.exp(jax.random.uniform(random_subkeys[3], (block_count, HEADS), jnp.float32, math.log(0.02), 0.0))
    quiet_rows = jnp.repeat(quiet_factor, BLOCK_TOKENS, axis=0)
    spike_length = max(3 * BLOCK_TOKENS // 8, 8)
    half_vocabulary = QUERY_WORDS // 2
    spike_offsets = jax.random.randint(random_subkeys[4], (2,), 0, half_vocabulary - spike_length + 1)
    spike_starts = spike_offsets + jnp.array([0, half_vocabulary], jnp.int32)
    token_positions = jnp.arange(QUERY_WORDS)[:, None]
    within_spike = jnp.any((token_positions >= spike_starts[None, :]) & (token_positions < spike_starts[None, :] + spike_length), axis=1).astype(jnp.float32)
    spike_step = 0.65 / (spike_length * 1.082)
    gradual_steps = (gradual_baseline[None, :] + spike_step * within_spike[:, None]) * jaggedness_level
    fast_steps = fast_base[None, :] * quiet_rows * jaggedness_level
    return jnp.where(is_slow[None, :], gradual_steps, fast_steps)


def shard_levels(key, extent, cuts, smallest, high):
    level = 1.0
    for dim, parts in cuts:
        draws = jax.random.uniform(jax.random.fold_in(jax.random.fold_in(key, 6), dim), (parts,), jnp.float32, smallest / len(cuts), high / len(cuts))
        level = level * jnp.repeat(jnp.exp(draws), extent[dim] // parts).reshape((-1,) + (1,) * (len(extent) - 1 - dim))
    return level


def bell_draw(stream_key, dims, scale, bound, shards=(), dtype=jnp.bfloat16):
    factor_of = shard_levels(stream_key, dims, shards, -0.22, 0.18) if shards else 1.0
    values = jax.random.normal(stream_key, dims, jnp.float32) * scale * factor_of
    return jnp.minimum(jnp.maximum(values, -bound), bound).astype(dtype)


def setup_inputs(seed: int = 0, part: int = 0) -> dict:
    arg_keys = jax.random.split(jax.random.key(seed), 13)
    part_keys = jax.random.split(jax.random.fold_in(arg_keys[12], part), 13)
    return {
        "heads_pre": bell_draw(part_keys[0], (QUERY_WORDS, HEADS * HEAD_DIM), 1.0, 6.0, ((0, 16), (1, 4))),
        "maps_pre": bell_draw(part_keys[1], (QUERY_WORDS, 2, GROUPS * STATE), 1.0, 6.0, ((0, 16), (2, 4))),
        "step_prompt": draw_step_prompt(jax.random.fold_in(jax.random.fold_in(arg_keys[12], part), 71), part),
        "head_rate": jnp.clip(jnp.exp(math.log(1.0) - 0.6931472 * jax.random.uniform(arg_keys[3], (HEADS,), jnp.float32) ** shard_levels(arg_keys[3], (HEADS,), ((0, 4),), -0.2, 0.2)), 0.5, 1.0),
        "skip_gain": jnp.clip(0.5 + 1.0 * jax.random.uniform(arg_keys[4], (HEADS,), jnp.float32) ** shard_levels(arg_keys[4], (HEADS,), ((0, 4),), -0.2, 0.2), 0.5, 1.5),
        "conv_head_taps": bell_draw(arg_keys[5], (CONV, HEADS * HEAD_DIM), CONV ** -0.5, 3.0, ((1, 4),), jnp.float32),
        "conv_head_bias": bell_draw(arg_keys[6], (HEADS * HEAD_DIM,), 0.5, 3.0, ((0, 4),), jnp.float32),
        "conv_map_taps": bell_draw(arg_keys[7], (CONV, 2, GROUPS * STATE), CONV ** -0.5, 3.0, ((2, 4),), jnp.float32),
        "filter_mapping_offset": bell_draw(arg_keys[8], (2, GROUPS * STATE), 0.5, 3.0, ((1, 4),), jnp.float32),
        "heads_dec": bell_draw(part_keys[9], (SAMPLES, STEPS, HEADS * HEAD_DIM), 1.0, 6.0, ((0, 16), (2, 4))),
        "maps_dec": bell_draw(part_keys[10], (SAMPLES, STEPS, 2, GROUPS * STATE), 1.0, 6.0, ((0, 16), (3, 4))),
        "step_dec": jnp.clip(jnp.exp(math.log(0.3) - 3.4011974 * jax.random.uniform(part_keys[11], (SAMPLES, STEPS, HEADS), jnp.float32) ** shard_levels(part_keys[11], (SAMPLES, STEPS, HEADS), ((0, 16), (2, 4)), -0.2, 0.2)), 0.01, 0.3),
    }


def conv_silu(padded, conv_weight, conv_bias, sequence_length):
    summed = conv_bias + conv_weight[0] * padded[0:sequence_length].astype(jnp.float32)
    for offset in range(1, CONV):
        summed = summed + conv_weight[offset] * padded[offset:offset + sequence_length].astype(jnp.float32)
    return jax.nn.silu(summed).astype(jnp.bfloat16)


def rounded(value):
    return lax.optimization_barrier(value.astype(jnp.bfloat16)).astype(jnp.float32)


def reference(heads_pre, maps_pre, step_prompt, head_rate, skip_gain, conv_head_taps, conv_head_bias, conv_map_taps, filter_mapping_offset, heads_dec, maps_dec, step_dec):
    per_group = HEADS // GROUPS
    x_conv = conv_silu(jnp.concatenate([jnp.zeros((CONV - 1, HEADS * HEAD_DIM), jnp.bfloat16), heads_pre], 0), conv_head_taps, conv_head_bias, QUERY_WORDS)
    bc_conv = conv_silu(jnp.concatenate([jnp.zeros((CONV - 1, 2, GROUPS * STATE), jnp.bfloat16), maps_pre], 0), conv_map_taps, filter_mapping_offset, QUERY_WORDS)
    blocks = QUERY_WORDS // BLOCK_TOKENS
    x_blocks = x_conv.reshape(blocks, BLOCK_TOKENS, GROUPS, per_group, HEAD_DIM)
    in_maps = bc_conv[:, 0].reshape(blocks, BLOCK_TOKENS, GROUPS, STATE)
    result_mappings = bc_conv[:, 1].reshape(blocks, BLOCK_TOKENS, GROUPS, STATE)
    step_block_list = step_prompt.reshape(blocks, BLOCK_TOKENS, GROUPS, per_group)
    decay_rate = head_rate.reshape(GROUPS, per_group)
    skip_heads = skip_gain.reshape(GROUPS, per_group)
    causal = jnp.arange(BLOCK_TOKENS)[:, None] >= jnp.arange(BLOCK_TOKENS)[None, :]

    def one_block(ssm_state, pieces):
        x_block, in_map, out_map, step_size = pieces
        log_decay = jnp.cumsum(-step_size * decay_rate, axis=0)
        log_columns = jnp.moveaxis(log_decay, 0, -1)
        logarithmic_spacings = log_columns[..., :, None] - log_columns[..., None, :]
        decay_mat = jnp.exp(jnp.where(causal, logarithmic_spacings, -jnp.inf))
        scores = jnp.einsum('qgn,sgn->gqs', out_map.astype(jnp.float32), in_map.astype(jnp.float32))
        mixing = rounded(scores[:, None] * decay_mat * jnp.moveaxis(step_size, 0, -1)[..., None, :])
        x_wide = x_block.astype(jnp.float32)
        y_inner = jnp.einsum('gjqs,sgjp->qgjp', mixing, x_wide)
        entry_low = rounded(ssm_state)
        y_cross = jnp.exp(log_decay)[..., None] * jnp.einsum('qgn,gjpn->qgjp', out_map.astype(jnp.float32), entry_low)
        output = (y_inner + y_cross + skip_heads[..., None] * x_wide).astype(jnp.bfloat16)
        weights = jnp.exp(log_decay[-1] - log_decay) * step_size
        weighted = rounded(x_wide * weights[..., None])
        block_state = jnp.einsum('qgjp,qgn->gjpn', weighted, in_map.astype(jnp.float32))
        ssm_state = jnp.exp(log_decay[-1])[..., None, None] * ssm_state + block_state
        return ssm_state, output

    start_state = jnp.zeros((GROUPS, per_group, HEAD_DIM, STATE), jnp.float32)
    final_state, outputs = lax.scan(one_block, start_state, (x_blocks, in_maps, result_mappings, step_block_list))
    prompt_out = outputs.reshape(QUERY_WORDS, HEADS * HEAD_DIM)
    tail_x = heads_pre[QUERY_WORDS - CONV + 1:]
    tail_bc = maps_pre[QUERY_WORDS - CONV + 1:]

    def one_sample(x_new, bc_new, step_new):
        dx_conv = conv_silu(jnp.concatenate([tail_x, x_new], 0), conv_head_taps, conv_head_bias, STEPS)
        dbc_conv = conv_silu(jnp.concatenate([tail_bc, bc_new], 0), conv_map_taps, filter_mapping_offset, STEPS)
        ssm_state = final_state
        rows_out = []
        for position in range(STEPS):
            x_step = dx_conv[position].reshape(GROUPS, per_group, HEAD_DIM).astype(jnp.float32)
            in_step = dbc_conv[position, 0].reshape(GROUPS, STATE).astype(jnp.float32)
            out_step = dbc_conv[position, 1].reshape(GROUPS, STATE).astype(jnp.float32)
            step_size = step_new[position].reshape(GROUPS, per_group)
            ssm_state = jnp.exp(-step_size * decay_rate)[..., None, None] * ssm_state + (step_size[..., None] * x_step)[..., None] * in_step[:, None, None, :]
            output = jnp.sum(ssm_state * out_step[:, None, None, :], axis=-1) + skip_heads[..., None] * x_step
            rows_out.append(output.astype(jnp.bfloat16).reshape(HEADS * HEAD_DIM))
        return jnp.stack(rows_out)

    sample_out = jax.vmap(one_sample)(heads_dec, maps_dec, step_dec)
    return prompt_out, sample_out
```

```python
import jax
import jax.numpy as jnp
from jax import lax
from jax.sharding import PartitionSpec as P

HEADS = 256
HEAD_DIM = 64
STATE = 256
GROUPS = 8
CONV = 4
BLOCK = 128
STEPS = 4
NEAR = 4
FAR = 4
NEAR_GROUPS = [[FAR_ * NEAR + i for i in range(NEAR)] for FAR_ in range(FAR)]
FAR_GROUPS = [[FAR_ * NEAR + i for FAR_ in range(FAR)] for i in range(NEAR)]
HL = 16
XC = HL * HEAD_DIM
f32 = jnp.float32
bf16 = jnp.bfloat16


def conv_silu(padded, taps, bias, length):
    summed = bias + taps[0] * padded[0:length].astype(f32)
    for offset in range(1, CONV):
        summed = summed + taps[offset] * padded[offset : offset + length].astype(f32)
    return jax.nn.silu(summed).astype(bf16)


def local(hp, mp, sp, rate, skip, ht, hb, mt, mb, hd, md, sd):
    me = lax.axis_index("seq")
    near = me % NEAR
    far = me // NEAR
    group = near // 2
    xin = jnp.concatenate([hp, hd[0]], 0).reshape(BLOCK + STEPS, NEAR, XC)
    maps = jnp.concatenate([mp, md[0]], 0).reshape(BLOCK + STEPS, 2, 2, STATE)
    maps = jnp.repeat(jnp.swapaxes(maps, 1, 2), 2, axis=1).reshape(BLOCK + STEPS, NEAR, 2 * STATE)
    packed = jnp.swapaxes(jnp.concatenate([xin, maps], -1), 0, 1)
    steps = jnp.concatenate([sp, sd[0]], 0).reshape(BLOCK + STEPS, NEAR, HL)
    steps = jnp.swapaxes(steps, 0, 1)
    packed = lax.all_to_all(packed, "seq", 0, 0, axis_index_groups=NEAR_GROUPS)
    steps = lax.all_to_all(steps, "seq", 0, 0, axis_index_groups=NEAR_GROUPS)

    pick = lambda a, axis, n: lax.dynamic_slice_in_dim(a, near * n, n, axis)
    rate = pick(rate, 0, HL)
    skip = pick(skip, 0, HL)
    mslice = lambda a: lax.dynamic_slice_in_dim(a, group * STATE, STATE, a.ndim - 1)
    taps = jnp.concatenate([pick(ht, 1, XC), mslice(mt).reshape(CONV, 2 * STATE)], 1)
    bias = jnp.concatenate([pick(hb, 0, XC), mslice(mb).reshape(2 * STATE)], 0)

    rows = packed[:, :BLOCK].reshape(NEAR * BLOCK, -1)
    ends = lax.all_gather(rows[-(CONV - 1) :], "seq", axis_index_groups=FAR_GROUPS)
    before = lax.dynamic_index_in_dim(ends, jnp.maximum(far - 1, 0), 0, keepdims=False)
    before = jnp.where(far > 0, before, jnp.zeros_like(before))
    tail = ends[FAR - 1]
    conv = conv_silu(jnp.concatenate([before, rows], 0), taps, bias, NEAR * BLOCK)
    xb = conv[:, :XC].reshape(NEAR, BLOCK, HL, HEAD_DIM)
    bm = conv[:, XC : XC + STATE].reshape(NEAR, BLOCK, STATE)
    cm = conv[:, XC + STATE :].reshape(NEAR, BLOCK, STATE)
    st = steps[:, :BLOCK]
    logd = jnp.cumsum(-st * rate, axis=1)
    last = logd[:, -1]
    weights = jnp.exp(last[:, None] - logd) * st
    weighted = (xb.astype(f32) * weights[..., None]).astype(bf16)
    bstate = jnp.einsum("cshp,csn->chpn", weighted, bm, preferred_element_type=f32)
    gains = jnp.exp(last)
    inner = [jnp.zeros_like(bstate[0])]
    lead = [jnp.ones_like(gains[0])]
    for c in range(NEAR):
        inner.append(gains[c][:, None, None] * inner[-1] + bstate[c])
        lead.append(lead[-1] * gains[c])
    all_states = lax.all_gather(inner[-1], "seq", axis_index_groups=FAR_GROUPS)
    all_leads = lax.all_gather(lead[-1], "seq", axis_index_groups=FAR_GROUPS)

    cols = jnp.moveaxis(logd, 1, -1)
    gap = cols[..., :, None] - cols[..., None, :]
    causal = jnp.arange(BLOCK)[:, None] >= jnp.arange(BLOCK)[None, :]
    decay = jnp.exp(jnp.where(causal, gap, -jnp.inf))
    scores = jnp.einsum("cqn,csn->cqs", cm, bm, preferred_element_type=f32)
    mixing = (scores[:, None] * decay * jnp.moveaxis(st, 1, -1)[..., None, :]).astype(bf16)
    y = jnp.einsum("chqs,cshp->cqhp", mixing, xb, preferred_element_type=f32)
    y = y + skip[:, None] * xb.astype(f32)

    drows = packed[:, BLOCK:]
    dpad = jnp.concatenate([jnp.broadcast_to(tail[None], (NEAR,) + tail.shape), drows], 1)
    dconv = jax.vmap(lambda p: conv_silu(p, taps, bias, STEPS))(dpad)
    dx = dconv[..., :XC].reshape(NEAR, STEPS, HL, HEAD_DIM).astype(f32)
    db = dconv[..., XC : XC + STATE]
    dc = dconv[..., XC + STATE :]
    ds = steps[:, BLOCK:]
    dlog = jnp.cumsum(-ds * rate, axis=1)
    dgap = dlog[:, :, None] - dlog[:, None, :]
    dcausal = jnp.arange(STEPS)[:, None] >= jnp.arange(STEPS)[None, :]
    ddecay = jnp.exp(jnp.where(dcausal[..., None], dgap, -jnp.inf)) * ds[:, None]
    dscore = jnp.sum(dc[:, :, None].astype(f32) * db[:, None].astype(f32), -1)
    dmix = dscore[..., None] * ddecay
    dy = jnp.sum(dmix[..., None] * dx[:, None], 2) + skip[:, None] * dx

    entry = jnp.zeros_like(all_states[0])
    state = jnp.zeros_like(entry)
    for g in range(FAR):
        state = all_leads[g][:, None, None] * state + all_states[g]
        entry = jnp.where(far == g + 1, state, entry)
    low = jnp.stack(
        [(lead[c][:, None, None] * entry + inner[c]).astype(bf16) for c in range(NEAR)]
    )
    cross = jnp.einsum("cqn,chpn->cqhp", cm, low, preferred_element_type=f32)
    out = (y + jnp.exp(logd)[..., None] * cross).astype(bf16).reshape(NEAR, BLOCK, XC)
    high = lax.reduce_precision(state, 8, 7)
    dcross = jnp.einsum("rkn,hpn->rkhp", dc, high.astype(bf16), preferred_element_type=f32)
    dcross = dcross + jnp.einsum(
        "rkn,hpn->rkhp", dc, (state - high).astype(bf16), preferred_element_type=f32
    )
    dout = (dy + jnp.exp(dlog)[..., None] * dcross).astype(bf16).reshape(NEAR, STEPS, XC)
    back = jnp.concatenate([out, dout], 1)
    back = lax.all_to_all(back, "seq", 0, 0, axis_index_groups=NEAR_GROUPS)
    back = jnp.swapaxes(back, 0, 1).reshape(BLOCK + STEPS, NEAR * XC)
    return back[:BLOCK], back[BLOCK:][None]


def solution(mesh):
    placed = (
        P(("prompt", "seq"), "head"),
        P(("prompt", "seq"), None, "head"),
        P(("prompt", "seq"), "head"),
        P("head"),
        P("head"),
        P(None, "head"),
        P("head"),
        P(None, None, "head"),
        P(None, "head"),
        P(("prompt", "seq"), None, "head"),
        P(("prompt", "seq"), None, None, "head"),
        P(("prompt", "seq"), None, "head"),
    )
    return jax.shard_map(
        local,
        mesh=mesh,
        in_specs=placed,
        out_specs=(P(("prompt", "seq"), "head"), P(("prompt", "seq"), None, "head")),
        check_vma=False,
    )
```
